32 devices in a mesh: slab: 16 (over z, y, core), head: 2 (over x).
Axes of the slice: x: 2, y: 2, z: 4, core: 2. Of those that a mesh axis runs over, the one named last changes fastest.
Arguments:
- queries: bfloat16 [8192, 1024], P('slab', 'head'), may hold values from -6.5 to 6.5
- key_values: bfloat16 [8192, 4096], P('slab', 'head'), may hold values from -6.5 to 6.5
- out_grads: bfloat16 [8192, 2560], P('slab', 'head'), may hold values from -6 to 6
- positions: float32 [3, 8192], P(None, 'slab'), may hold values from 0 to 4, as said below
- counts: int32 [16], P('slab'), may hold values from 384 to 512, as said below
- gamma: float32 [16], P('head'), may hold values from 0.05 to 1
Outputs:
- query_grads: bfloat16 [8192, 1024], P('slab', 'head')
- key_value_grads: bfloat16 [8192, 4096], P('slab', 'head')
- position_grads: float32 [3, 8192], P(None, 'slab')
The draws below stay inside these ranges and needn't reach their ends.
Inputs may be any that keep to these rules, and one draw needn't show every extreme that they name: `positions`: row 0 is x within the atom's own slab, from 0 to 1; rows 1 and 2 are y and z, from 0 to 4. `counts`: real atoms fill the first rows of their slab; some slab holds exactly 512 real atoms in every draw.
All inputs are finite; a program needn't handle non-finite values.
Results may differ from the reference program's by a relative error of at most 0.01.
Values may be sent and summed in bfloat16 or wider, within the bound.
A program may use at most 256 MiB of HBM per device.

```python
import math
import jax
import jax.numpy as jnp
from jax import lax

ROWS = 512
HEADS = 16
HEAD_DIM = 64
VEC = 32
SLABS = 16
ATOMS = 8192


def draw_queries(key, part):
    shape = (ATOMS, HEADS, HEAD_DIM)
    result = jnp.clip(jax.random.normal(jax.random.fold_in(key, 11), shape), -6.0, 6.0)
    return result.reshape(ATOMS, HEADS * HEAD_DIM).astype(jnp.bfloat16)


def draw_key_values(key, part):
    key_shape = (ATOMS, HEADS, HEAD_DIM)
    value_shape = (ATOMS, HEADS, HEAD_DIM + 4 * VEC)
    key_part = jnp.clip(jax.random.normal(jax.random.fold_in(key, 21), key_shape), -6.0, 6.0)
    value_part = jnp.clip(jax.random.normal(jax.random.fold_in(key, 22), value_shape), -6.0, 6.0)
    joined = jnp.concatenate([key_part, value_part], axis=2)
    return joined.reshape(ATOMS, HEADS * (2 * HEAD_DIM + 4 * VEC)).astype(jnp.bfloat16)


def draw_positions(key, part):
    unit = jax.random.uniform(jax.random.fold_in(key, 31), (3, ATOMS))
    spans = jnp.array([1.0, 4.0, 4.0], jnp.float32)[:, None]
    placed = unit * spans
    return placed.astype(jnp.float32)


def draw_counts(key, part):
    short_by = jax.random.randint(jax.random.fold_in(key, 41), (SLABS,), 0, ROWS // 4 + 1)
    full_slab = jax.random.randint(jax.random.fold_in(key, 42), (), 0, SLABS)
    slab_ids = jnp.arange(SLABS)
    return jnp.where(slab_ids == full_slab, ROWS, ROWS - short_by).astype(jnp.int32)


def levels(rng, shape, split, smallest, top_value):
    level, own = 1.0, jax.random.fold_in(rng, 6)
    for dim, blocks in split:
        draws = jnp.exp(jax.random.uniform(jax.random.fold_in(own, dim), (blocks,), jnp.float32, smallest / len(split), top_value / len(split)))
        level = level * jnp.repeat(draws, shape[dim] // blocks).reshape([-1 if axis == dim else 1 for axis in range(len(shape))])
    return level


def normal_values(own_key, dims, scale, reach, cuts=(), kind=jnp.bfloat16):
    factor_of = levels(own_key, dims, cuts, -0.22, 0.18) if cuts else 1.0
    values = jax.random.normal(own_key, dims, jnp.float32) * scale * factor_of
    return jnp.minimum(jnp.maximum(values, -reach), reach).astype(kind)


def setup_inputs(seed: int = 0) -> dict:
    keys = jax.random.split(jax.random.key(seed), 7)
    return {
        "queries": draw_queries(jax.random.fold_in(keys[6], 71), 0),
        "key_values": draw_key_values(jax.random.fold_in(keys[6], 71), 0),
        "out_grads": normal_values(keys[2], (ATOMS, HEADS * (HEAD_DIM + 3 * VEC)), 1.0, 6.0, ((0, 16), (1, 2))),
        "positions": draw_positions(jax.random.fold_in(keys[6], 71), 0),
        "counts": draw_counts(jax.random.fold_in(keys[6], 71), 0),
        "gamma": jnp.clip(jnp.exp(math.log(1.0) - 2.9957323 * jax.random.uniform(keys[5], (HEADS,), jnp.float32) ** levels(keys[5], (HEADS,), ((0, 2),), -0.2, 0.2)), 0.05, 1.0),
    }


score_scale = 0.125
radius_factor = 0.25
envelope_rate = 0.5
negative_fill = -1.0e30


def cross_dot(first_op, second_op):
    return lax.dot_general(first_op, second_op, (((1,), (1,)), ((), ())), preferred_element_type=jnp.float32)


def back_dot(first_op, second_op):
    return lax.dot_general(first_op, second_op, (((0,), (0,)), ((), ())), preferred_element_type=jnp.float32)


def prime_values(key_block, key_coords, offset):
    values = key_block[:, HEAD_DIM:].astype(jnp.float32)
    gate_values = values[:, HEAD_DIM + 3 * VEC:]
    frames = (key_coords[0] + offset, key_coords[1], key_coords[2])
    pieces = [values[:, :HEAD_DIM]]
    for component in range(3):
        column = HEAD_DIM + component * VEC
        pieces.append(values[:, column:column + VEC] + frames[component][:, None] * gate_values)
    pieces.append(gate_values)
    return jnp.concatenate(pieces, axis=1).astype(jnp.bfloat16)


def prime_grads(cotangent_rows, coords):
    values = cotangent_rows.astype(jnp.float32)
    gate_tail = jnp.zeros((values.shape[0], VEC), jnp.float32)
    for component in range(3):
        column = HEAD_DIM + component * VEC
        gate_tail = gate_tail - coords[component][:, None] * values[:, column:column + VEC]
    joined = jnp.concatenate([values, gate_tail], axis=1) * coords[3][:, None]
    return joined.astype(jnp.bfloat16)


def geometry(query_coords, key_coords, offset):
    shift_x = (key_coords[0] + offset)[None, :] - query_coords[0][:, None]
    shift_y = key_coords[1][None, :] - query_coords[1][:, None]
    shift_z = key_coords[2][None, :] - query_coords[2][:, None]
    distance = shift_x * shift_x + shift_y * shift_y + shift_z * shift_z
    inside = 1.0 - distance * radius_factor
    pair_mask = (inside > 0.0) & (key_coords[3][None, :] > 0.5)
    return distance, inside, pair_mask


def pair_scores(query_rows, key_rows, head_gamma, distance):
    return cross_dot(query_rows, key_rows) * score_scale - head_gamma * distance


def head_terms(query_rows, query_coords, cotangent, blocks, head_gamma):
    row_count = query_rows.shape[0]
    row_max = jnp.full((row_count,), negative_fill, jnp.float32)
    for offset, key_rows, primed, key_coords in blocks:
        distance, inside, pair_mask = geometry(query_coords, key_coords, offset)
        scores = pair_scores(query_rows, key_rows, head_gamma, distance)
        row_max = jnp.maximum(row_max, jnp.max(jnp.where(pair_mask, scores, negative_fill), axis=1))
    totals = 1.0 - query_coords[3]
    weighted = jnp.zeros((row_count,), jnp.float32)
    for offset, key_rows, primed, key_coords in blocks:
        distance, inside, pair_mask = geometry(query_coords, key_coords, offset)
        scores = pair_scores(query_rows, key_rows, head_gamma, distance)
        exponent = jnp.where(pair_mask, jnp.exp(scores - row_max[:, None]), 0.0)
        weight = inside * inside * exponent
        totals = totals + jnp.sum(weight, axis=1)
        weighted = weighted + jnp.sum(weight * cross_dot(cotangent, primed), axis=1)
    deltas = weighted / totals
    recip = 1.0 / totals
    query_grad = jnp.zeros((row_count, HEAD_DIM), jnp.float32)
    query_pos = jnp.zeros((3, row_count), jnp.float32)
    gate_sum = jnp.zeros((row_count, VEC), jnp.float32)
    block_terms = []
    gate_start = HEAD_DIM + 3 * VEC
    for offset, key_rows, primed, key_coords in blocks:
        distance, inside, pair_mask = geometry(query_coords, key_coords, offset)
        scores = pair_scores(query_rows, key_rows, head_gamma, distance)
        exponent = jnp.where(pair_mask, jnp.exp(scores - row_max[:, None]), 0.0)
        weight = inside * inside * exponent
        spread = cross_dot(cotangent, primed) - deltas[:, None]
        attend = weight * recip[:, None]
        dscore = attend * spread
        pulling = -head_gamma * dscore - envelope_rate * inside * exponent * recip[:, None] * spread
        dscore_b = dscore.astype(jnp.bfloat16)
        attend_b = attend.astype(jnp.bfloat16)
        query_grad = query_grad + jnp.dot(dscore_b, key_rows, preferred_element_type=jnp.float32)
        key_grad = back_dot(dscore_b, query_rows) * score_scale
        primed_grad = back_dot(attend_b, cotangent)
        gate_values = primed[:, gate_start:]
        gate_sum = gate_sum + jnp.dot(attend_b, gate_values, preferred_element_type=jnp.float32)
        frames = jnp.stack([key_coords[0] + offset, key_coords[1], key_coords[2]])
        row_pull = jnp.sum(pulling, axis=1)
        col_pull = jnp.sum(pulling, axis=0)
        query_side = jnp.einsum("ij,cj->ci", pulling, frames, precision=lax.Precision.HIGHEST)
        key_side = jnp.einsum("ij,ci->cj", pulling, query_coords[:3], precision=lax.Precision.HIGHEST)
        query_pos = query_pos - 2.0 * (query_side - query_coords[:3] * row_pull[None, :])
        gate_float = gate_values.astype(jnp.float32)
        value_pos = []
        gate_grad = primed_grad[:, gate_start:]
        for component in range(3):
            column = HEAD_DIM + component * VEC
            piece = primed_grad[:, column:column + VEC]
            value_pos.append(jnp.sum(gate_float * piece, axis=1))
            gate_grad = gate_grad + frames[component][:, None] * piece
        key_pos = 2.0 * (frames * col_pull[None, :] - key_side) + jnp.stack(value_pos)
        view_term = jnp.concatenate([key_grad, primed_grad[:, :gate_start], gate_grad], axis=1)
        block_terms.append((view_term, key_pos))
    cot_float = cotangent.astype(jnp.float32)
    extra = []
    for component in range(3):
        column = HEAD_DIM + component * VEC
        extra.append(jnp.sum(cot_float[:, column:column + VEC] * gate_sum, axis=1))
    query_pos = query_pos - jnp.stack(extra)
    return query_grad * score_scale, query_pos, block_terms


def reference(queries, key_values, out_grads, positions, counts, gamma):
    slab_count = counts.shape[0]
    block_width = 2 * HEAD_DIM + 4 * VEC
    cot_width = HEAD_DIM + 3 * VEC
    row_ids = jnp.arange(ROWS, dtype=jnp.int32)
    validity = (row_ids[None, :] < counts[:, None]).astype(jnp.float32)
    coords = jnp.concatenate([positions.reshape(3, slab_count, ROWS).transpose(1, 0, 2), validity[:, None, :]], axis=1)
    query_heads = queries.reshape(slab_count, ROWS, HEADS, HEAD_DIM).transpose(2, 0, 1, 3)
    kv_heads = key_values.reshape(slab_count, ROWS, HEADS, block_width).transpose(2, 0, 1, 3)
    cot_heads = out_grads.reshape(slab_count, ROWS, HEADS, cot_width).transpose(2, 0, 1, 3)

    def one_head(packed):
        query_all, kv_all, cot_all, head_gamma = packed

        def visit_slab(carried, slab_index):
            kv_acc, pos_acc = carried
            own_coords = coords[slab_index]
            cotangent = prime_grads(cot_all[slab_index], own_coords)
            blocks = []
            owners = []
            for offset in (-2, -1, 0, 1, 2):
                owner_slab = ((slab_index + offset) % slab_count).astype(jnp.int32)
                key_block = kv_all[owner_slab]
                key_coords = coords[owner_slab]
                blocks.append((offset, key_block[:, :HEAD_DIM], prime_values(key_block, key_coords, offset), key_coords))
                owners.append(owner_slab)
            query_grad, query_pos, block_terms = head_terms(query_all[slab_index], own_coords, cotangent, blocks, head_gamma)
            pos_acc = pos_acc.at[slab_index].add(query_pos)
            for owner_slab, (view_term, key_pos) in zip(owners, block_terms):
                kv_acc = kv_acc.at[owner_slab].add(view_term)
                pos_acc = pos_acc.at[owner_slab].add(key_pos)
            return (kv_acc, pos_acc), query_grad

        start = (jnp.zeros((slab_count, ROWS, block_width), jnp.float32), jnp.zeros((slab_count, 3, ROWS), jnp.float32))
        (kv_acc, pos_acc), query_grad = lax.scan(visit_slab, start, jnp.arange(slab_count, dtype=jnp.int32))
        return query_grad.astype(jnp.bfloat16), kv_acc.astype(jnp.bfloat16), pos_acc

    query_out, kv_out, pos_out = lax.map(one_head, (query_heads, kv_heads, cot_heads, gamma))
    query_grads = query_out.transpose(1, 2, 0, 3).reshape(slab_count * ROWS, HEADS * HEAD_DIM)
    key_value_grads = kv_out.transpose(1, 2, 0, 3).reshape(slab_count * ROWS, HEADS * block_width)
    position_grads = jnp.sum(pos_out, axis=0).transpose(1, 0, 2).reshape(3, slab_count * ROWS)
    return query_grads, key_value_grads, position_grads
```

```python
import functools

import jax
import jax.numpy as jnp
from jax import lax
from jax.experimental import pallas as pl
from jax.experimental.pallas import tpu as pltpu
from jax.sharding import PartitionSpec as P

HEAD_DIM = 64
VEC = 32
WIDTH = 2 * HEAD_DIM + 4 * VEC
COT = HEAD_DIM + 3 * VEC
OFFSETS = (-2, -1, 0, 1, 2)
FAR = 1e6
FLOOR = -1e4
CHUNK = 256
GROUPS = 2


def passed_along(block, axis, distance):
    count = lax.axis_size(axis)
    route = [((i - distance) % count, i) for i in range(count)]
    return lax.ppermute(block, axis, route)


def dot_nt(a, b):
    return lax.dot_general(a, b, (((1,), (1,)), ((), ())), preferred_element_type=jnp.float32)


def dot_tn(a, b):
    return lax.dot_general(a, b, (((0,), (0,)), ((), ())), preferred_element_type=jnp.float32)


def dot_nn(a, b):
    return jnp.dot(a, b, preferred_element_type=jnp.float32)


def spread_groups(x):
    x = x + pltpu.roll(x, 2 * VEC, 1)
    return x + pltpu.roll(x, VEC, 1)


def folded(x):
    return jnp.sum(x.reshape(x.shape[0] // 8, 8, x.shape[1]), axis=0)


def kernel(gamma_ref, q_ref, c_ref, ct_ref, qc_ref, kc_ref, *rest):
    views = len(OFFSETS)
    kv_refs = rest[:views]
    t_refs = rest[views : 2 * views]
    dq_ref, kp_ref, qp_ref = rest[2 * views : 2 * views + 3]
    dist, pair, dpair, pull, gates, frames, vpos, qpos = rest[2 * views + 3 :]
    rows = q_ref.shape[1]
    chunks = rows // CHUNK
    step = pl.program_id(0)
    head_gamma = gamma_ref[step]
    lane = lax.broadcasted_iota(jnp.int32, (CHUNK, 4 * VEC), 1)
    last_group = lane >= 3 * VEC

    @pl.when(step == 0)
    def _():
        vpos[...] = jnp.zeros_like(vpos)
        qpos[...] = jnp.zeros_like(qpos)

        @pl.loop(0, views * chunks)
        def _(k):
            at = pl.ds(pl.multiple_of(k * CHUNK, CHUNK), CHUNK)
            kc = kc_ref[at, :]
            total = None
            for c in range(3):
                shift = kc[:, c : c + 1] - qc_ref[c : c + 1, :]
                total = shift * shift if total is None else total + shift * shift
            counted = (1.0 - total * 0.25 > 0.0) & (kc[:, 3:4] > 0.5)
            dist[at, :] = jnp.where(counted, total, FAR)
            pull[at, :] = jnp.zeros((CHUNK, rows), jnp.float32)
            frames[at, :] = jnp.where(
                lane < VEC,
                kc[:, 0:1],
                jnp.where(lane < 2 * VEC, kc[:, 1:2], jnp.where(last_group, 0.0, kc[:, 2:3])),
            )

    q = q_ref[0]
    cot = c_ref[0]
    peak = jnp.full((8, rows), FLOOR, jnp.float32)
    for v in range(views):

        def scored(k, peak, v=v):
            off = pl.multiple_of(k * CHUNK, CHUNK)
            at = pl.ds(v * rows + off, CHUNK)
            s = dot_nt(kv_refs[v][pl.ds(off, CHUNK), : 2 * HEAD_DIM], q[:, : 2 * HEAD_DIM])
            s = s - head_gamma * dist[at, :]
            pair[at, :] = s
            return jnp.maximum(peak, jnp.max(s.reshape(CHUNK // 8, 8, rows), axis=0))

        peak = lax.fori_loop(0, chunks, scored, peak, unroll=True)
    peak = jnp.max(peak, axis=0, keepdims=True)

    totals = jnp.zeros((8, rows), jnp.float32)
    weighted = jnp.zeros((8, rows), jnp.float32)
    for v in range(views):

        def summed(k, carry, v=v):
            totals, weighted = carry
            off = pl.multiple_of(k * CHUNK, CHUNK)
            at = pl.ds(v * rows + off, CHUNK)
            kv = kv_refs[v][pl.ds(off, CHUNK), :]
            high = kv[:, 2 * HEAD_DIM :].astype(jnp.float32)
            gate = spread_groups(jnp.where(last_group, high, 0.0))
            gates[at, :] = gate
            primed = (high + frames[at, :] * gate).astype(jnp.bfloat16)
            dp = dot_nt(kv[:, : 2 * HEAD_DIM], cot[:, : 2 * HEAD_DIM]) + dot_nt(
                primed, cot[:, 2 * HEAD_DIM :]
            )
            inside = 1.0 - 0.25 * dist[at, :]
            part = inside * jnp.exp(pair[at, :] - peak)
            pair[at, :] = part
            dpair[at, :] = dp
            weight = inside * part
            return totals + folded(weight), weighted + folded(weight * dp)

        totals, weighted = lax.fori_loop(0, chunks, summed, (totals, weighted), unroll=True)
    total = jnp.sum(totals, axis=0, keepdims=True) + (1.0 - qc_ref[3:4, :])
    recip = 1.0 / total
    delta = jnp.sum(weighted, axis=0, keepdims=True) / total

    dq = jnp.zeros((2 * HEAD_DIM, rows), jnp.float32)
    gsum = jnp.zeros((4 * VEC, rows), jnp.float32)
    for v in range(views):

        def graded(k, carry, v=v):
            dq, gsum = carry
            off = pl.multiple_of(k * CHUNK, CHUNK)
            at = pl.ds(v * rows + off, CHUNK)
            here = pl.ds(off, CHUNK)
            inside = 1.0 - 0.25 * dist[at, :]
            unit = pair[at, :] * recip
            moved = unit * (dpair[at, :] - delta)
            dscore = inside * moved
            pull[at, :] += head_gamma * dscore + 0.5 * moved
            dscore_b = dscore.astype(jnp.bfloat16)
            attend_b = (inside * unit).astype(jnp.bfloat16)
            term = dot_nn(dscore_b, q) + dot_nn(attend_b, cot)
            kv = kv_refs[v][here, :]
            dq = dq + dot_tn(kv[:, : 2 * HEAD_DIM], dscore_b)
            gsum = gsum + dot_tn(kv[:, 2 * HEAD_DIM :], attend_b)
            high = term[:, 2 * HEAD_DIM :]
            vpos[at, :] += gates[at, :] * high
            extra = spread_groups(frames[at, :] * high)
            high = high + jnp.where(last_group, extra, 0.0)
            t_refs[v][here, : 2 * HEAD_DIM] = term[:, : 2 * HEAD_DIM].astype(t_refs[v].dtype)
            t_refs[v][here, 2 * HEAD_DIM :] = high.astype(t_refs[v].dtype)
            return dq, gsum

        dq, gsum = lax.fori_loop(0, chunks, graded, (dq, gsum), unroll=True)
    dq_ref[...] = (dq[:HEAD_DIM, :] * 0.125).astype(dq_ref.dtype)
    gsum = gsum[3 * VEC :, :]
    for c in range(3):
        part = ct_ref[0, c * VEC : (c + 1) * VEC, :].astype(jnp.float32) * gsum
        qpos[c : c + 1, :] -= jnp.sum(part, axis=0, keepdims=True)

    @pl.when(step == pl.num_programs(0) - 1)
    def _():
        def placed(k, sums):
            at = pl.ds(pl.multiple_of(k * CHUNK, CHUNK), CHUNK)
            kc = kc_ref[at, :]
            force = -2.0 * pull[at, :]
            vp = vpos[at, :]
            out = []
            cols = []
            for c in range(3):
                moment = force * (kc[:, c : c + 1] - qc_ref[c : c + 1, :])
                out.append(sums[c] - folded(moment))
                mine = (lane >= c * VEC) & (lane < (c + 1) * VEC)
                col = jnp.sum(moment, axis=1, keepdims=True)
                cols.append(col + jnp.sum(jnp.where(mine, vp, 0.0), axis=1, keepdims=True))
            kp_ref[at, :] = jnp.concatenate(cols + [jnp.zeros_like(cols[0])], axis=1)
            return tuple(out)

        zero = jnp.zeros((8, rows), jnp.float32)
        sums = lax.fori_loop(0, views * chunks, placed, (zero, zero, zero))
        qp_ref[...] = qpos[...]
        for c in range(3):
            qp_ref[c : c + 1, :] += jnp.sum(sums[c], axis=0, keepdims=True)


def head_group(gamma, q, cot, cot_t, query_coords, key_coords, blocks):
    heads, rows, _ = q.shape
    views = len(OFFSETS)
    keys = views * rows
    f32 = jnp.float32
    per_head = lambda h: (h, 0, 0)
    whole = lambda h: (0, 0)
    column = lambda h: (0, h)
    return pl.pallas_call(
        kernel,
        grid=(heads,),
        in_specs=[
            pl.BlockSpec(memory_space=pltpu.SMEM),
            pl.BlockSpec((1, rows, WIDTH), per_head),
            pl.BlockSpec((1, rows, WIDTH), per_head),
            pl.BlockSpec((1, 3 * VEC, rows), per_head),
            pl.BlockSpec(query_coords.shape, whole),
            pl.BlockSpec(key_coords.shape, whole),
        ]
        + [pl.BlockSpec((rows, WIDTH), column)] * views,
        out_specs=[pl.BlockSpec((rows, WIDTH), column)] * views
        + [
            pl.BlockSpec((HEAD_DIM, rows), lambda h: (h, 0)),
            pl.BlockSpec((keys, 4), whole),
            pl.BlockSpec((8, rows), whole),
        ],
        out_shape=[jax.ShapeDtypeStruct((rows, heads * WIDTH), jnp.bfloat16)] * views
        + [
            jax.ShapeDtypeStruct((heads * HEAD_DIM, rows), jnp.bfloat16),
            jax.ShapeDtypeStruct((keys, 4), f32),
            jax.ShapeDtypeStruct((8, rows), f32),
        ],
        scratch_shapes=[
            pltpu.VMEM((keys, rows), f32),
            pltpu.VMEM((keys, rows), f32),
            pltpu.VMEM((keys, rows), f32),
            pltpu.VMEM((keys, rows), f32),
            pltpu.VMEM((keys, 4 * VEC), f32),
            pltpu.VMEM((keys, 4 * VEC), f32),
            pltpu.VMEM((keys, 4 * VEC), f32),
            pltpu.VMEM((8, rows), f32),
        ],
        compiler_params=pltpu.CompilerParams(
            dimension_semantics=("arbitrary",), vmem_limit_bytes=60 * 2**20
        ),
        cost_estimate=pl.CostEstimate(
            flops=heads * rows * keys * 1500,
            bytes_accessed=heads * keys * WIDTH * 4,
            transcendentals=heads * rows * keys,
        ),
        name="pairs",
    )(gamma, q, cot, cot_t, query_coords, key_coords, *blocks)


def per_device(queries, key_values, out_grads, positions, counts, gamma):
    rows = queries.shape[0]
    heads = gamma.shape[0]
    groups = GROUPS if heads % GROUPS == 0 else 1
    size = heads // groups
    f32 = jnp.float32
    bf16 = jnp.bfloat16
    validity = (jnp.arange(rows, dtype=jnp.int32) < counts[0]).astype(f32)
    coords = jnp.concatenate([positions, validity[None, :]], axis=0)
    coords_at = {0: coords}
    for o in (1, -1, 2, -2):
        coords_at[o] = passed_along(coords, "slab", -o)

    pieces = [key_values[:, g * size * WIDTH : (g + 1) * size * WIDTH] for g in range(groups)]
    fetched = []
    for g in range(groups):
        blocks = {0: pieces[g]}
        for o in (1, -1):
            blocks[o] = passed_along(blocks[0], "slab", -o)
        for o in (1, -1):
            blocks[2 * o] = passed_along(blocks[o], "slab", -o)
        fetched.append(blocks)

    q = queries.reshape(rows, heads, HEAD_DIM).transpose(1, 0, 2) * bf16(0.125)
    q = jnp.pad(q, ((0, 0), (0, 0), (0, WIDTH - HEAD_DIM)))
    do = out_grads.reshape(rows, heads, COT).transpose(1, 0, 2).astype(f32)
    tail = jnp.zeros((heads, rows, VEC), f32)
    for c in range(3):
        at = HEAD_DIM + c * VEC
        tail = tail - coords[c][None, :, None] * do[:, :, at : at + VEC]
    cot = jnp.concatenate([do, tail], axis=2) * validity[None, :, None]
    cot = jnp.pad(cot, ((0, 0), (0, 0), (HEAD_DIM, 0))).astype(bf16)
    cot_t = cot[:, :, 2 * HEAD_DIM : 2 * HEAD_DIM + 3 * VEC].transpose(0, 2, 1)

    query_coords = jnp.pad(coords, ((0, 4), (0, 0)))
    key_coords = jnp.concatenate(
        [coords_at[o] + jnp.array([o, 0, 0, 0], f32)[:, None] for o in OFFSETS], axis=1
    ).T

    dq_parts = []
    kv_parts = []
    key_pos = 0.0
    query_pos = 0.0
    for g in range(groups):
        part = slice(g * size, (g + 1) * size)
        out = head_group(
            gamma[part], q[part], cot[part], cot_t[part], query_coords, key_coords,
            [fetched[g][o] for o in OFFSETS],
        )
        terms = dict(zip(OFFSETS, out[: len(OFFSETS)]))
        dq_parts.append(out[-3])
        key_pos = key_pos + out[-2]
        query_pos = query_pos + out[-1][:3]
        collected = terms[0].astype(f32)
        for o in (1, -1):
            moving = passed_along(terms[2 * o], "slab", o)
            moving = (moving.astype(f32) + terms[o].astype(f32)).astype(bf16)
            collected = collected + passed_along(moving, "slab", o).astype(f32)
        kv_parts.append(collected.astype(bf16))

    key_pos = key_pos.T[:3].reshape(3, len(OFFSETS), rows)
    total = query_pos
    for n, o in enumerate(OFFSETS):
        total = total + (key_pos[:, n] if o == 0 else passed_along(key_pos[:, n], "slab", o))
    position_grads = lax.psum(total, "head")
    query_grads = jnp.concatenate(dq_parts, axis=0).T
    return (query_grads, jnp.concatenate(kv_parts, axis=1), position_grads)


def solution(mesh):
    in_specs = (
        P("slab", "head"),
        P("slab", "head"),
        P("slab", "head"),
        P(None, "slab"),
        P("slab"),
        P("head"),
    )
    out_specs = (P("slab", "head"), P("slab", "head"), P(None, "slab"))
    return jax.shard_map(
        per_device, mesh=mesh, in_specs=in_specs, out_specs=out_specs, check_vma=False
    )
```

```python
import functools

import jax
import jax.numpy as jnp
from jax import lax
from jax.experimental import pallas as pl
from jax.experimental.pallas import tpu as pltpu
from jax.sharding import PartitionSpec as P

HEAD_DIM = 64
VEC = 32
WIDTH = 2 * HEAD_DIM + 4 * VEC
COT = HEAD_DIM + 3 * VEC
VIEWS = 5
FAR = 1e6
FLOOR = -1e4
CHUNK = 256
GROUPS = 4


def routed(block, axis, target):
    route = [(i, target(i) % lax.axis_size(axis)) for i in range(lax.axis_size(axis))]
    return lax.ppermute(block, axis, route)


def across_pairs(block):
    return routed(block, "slab", lambda i: i ^ 2)


def along_line(block, sign):
    return routed(block, "slab", lambda i: i + (sign if i & 2 == 0 else -sign) * 4)


def across_cores(block):
    return routed(block, "slab", lambda i: i ^ 1)


def fetched_views(block, near):
    far_one = across_pairs(block)
    far_two = along_line(far_one, 1)
    next_one = across_cores(block)
    next_two = across_cores(jnp.where(near, far_one, far_two))
    return [block, far_one, far_two, next_one, next_two]


def returned_terms(terms, near, dtype):
    f32 = jnp.float32
    own, far_one, far_two, next_one, next_two = terms
    swapped = across_cores(next_two).astype(f32)
    far_two = far_two.astype(f32) + jnp.where(near, 0.0, swapped)
    far_one = far_one.astype(f32) + jnp.where(near, swapped, 0.0)
    far_one = far_one + along_line(far_two.astype(dtype), -1).astype(f32)
    own = own.astype(f32) + across_cores(next_one).astype(f32)
    return own + across_pairs(far_one.astype(dtype)).astype(f32)


def dot_nt(a, b):
    return lax.dot_general(a, b, (((1,), (1,)), ((), ())), preferred_element_type=jnp.float32)


def dot_tn(a, b):
    return lax.dot_general(a, b, (((0,), (0,)), ((), ())), preferred_element_type=jnp.float32)


def dot_nn(a, b):
    return jnp.dot(a, b, preferred_element_type=jnp.float32)


def spread_groups(x):
    x = x + pltpu.roll(x, 2 * VEC, 1)
    return x + pltpu.roll(x, VEC, 1)


def folded(x):
    return jnp.sum(x.reshape(x.shape[0] // 8, 8, x.shape[1]), axis=0)


def kernel(gamma_ref, q_ref, c_ref, ct_ref, qc_ref, kc_ref, *rest):
    views = VIEWS
    kv_refs = rest[:views]
    t_refs = rest[views : 2 * views]
    dq_ref, kp_ref, qp_ref = rest[2 * views : 2 * views + 3]
    dist, pair, dpair, pull, gates, frames, vpos, qpos = rest[2 * views + 3 :]
    rows = q_ref.shape[1]
    chunks = rows // CHUNK
    step = pl.program_id(0)
    head_gamma = gamma_ref[step]
    lane = lax.broadcasted_iota(jnp.int32, (CHUNK, 4 * VEC), 1)
    last_group = lane >= 3 * VEC

    @pl.when(step == 0)
    def _():
        vpos[...] = jnp.zeros_like(vpos)
        qpos[...] = jnp.zeros_like(qpos)

        @pl.loop(0, views * chunks)
        def _(k):
            at = pl.ds(pl.multiple_of(k * CHUNK, CHUNK), CHUNK)
            kc = kc_ref[at, :]
            total = None
            for c in range(3):
                shift = kc[:, c : c + 1] - qc_ref[c : c + 1, :]
                total = shift * shift if total is None else total + shift * shift
            counted = (1.0 - total * 0.25 > 0.0) & (kc[:, 3:4] > 0.5)
            dist[at, :] = jnp.where(counted, total, FAR)
            pull[at, :] = jnp.zeros((CHUNK, rows), jnp.float32)
            frames[at, :] = jnp.where(
                lane < VEC,
                kc[:, 0:1],
                jnp.where(lane < 2 * VEC, kc[:, 1:2], jnp.where(last_group, 0.0, kc[:, 2:3])),
            )

    q = q_ref[0]
    cot = c_ref[0]
    peak = jnp.full((8, rows), FLOOR, jnp.float32)
    for v in range(views):

        def scored(k, peak, v=v):
            off = pl.multiple_of(k * CHUNK, CHUNK)
            at = pl.ds(v * rows + off, CHUNK)
            s = dot_nt(kv_refs[v][pl.ds(off, CHUNK), : 2 * HEAD_DIM], q[:, : 2 * HEAD_DIM])
            s = s - head_gamma * dist[at, :]
            pair[at, :] = s
            return jnp.maximum(peak, jnp.max(s.reshape(CHUNK // 8, 8, rows), axis=0))

        peak = lax.fori_loop(0, chunks, scored, peak, unroll=True)
    peak = jnp.max(peak, axis=0, keepdims=True)

    totals = jnp.zeros((8, rows), jnp.float32)
    weighted = jnp.zeros((8, rows), jnp.float32)
    for v in range(views):

        def summed(k, carry, v=v):
            totals, weighted = carry
            off = pl.multiple_of(k * CHUNK, CHUNK)
            at = pl.ds(v * rows + off, CHUNK)
            kv = kv_refs[v][pl.ds(off, CHUNK), :]
            high = kv[:, 2 * HEAD_DIM :].astype(jnp.float32)
            gate = spread_groups(jnp.where(last_group, high, 0.0))
            gates[at, :] = gate
            primed = (high + frames[at, :] * gate).astype(jnp.bfloat16)
            dp = dot_nt(kv[:, : 2 * HEAD_DIM], cot[:, : 2 * HEAD_DIM]) + dot_nt(
                primed, cot[:, 2 * HEAD_DIM :]
            )
            inside = 1.0 - 0.25 * dist[at, :]
            part = inside * jnp.exp(pair[at, :] - peak)
            pair[at, :] = part
            dpair[at, :] = dp
            weight = inside * part
            return totals + folded(weight), weighted + folded(weight * dp)

        totals, weighted = lax.fori_loop(0, chunks, summed, (totals, weighted), unroll=True)
    total = jnp.sum(totals, axis=0, keepdims=True) + (1.0 - qc_ref[3:4, :])
    recip = 1.0 / total
    delta = jnp.sum(weighted, axis=0, keepdims=True) / total

    dq = jnp.zeros((2 * HEAD_DIM, rows), jnp.float32)
    gsum = jnp.zeros((4 * VEC, rows), jnp.float32)
    for v in range(views):

        def graded(k, carry, v=v):
            dq, gsum = carry
            off = pl.multiple_of(k * CHUNK, CHUNK)
            at = pl.ds(v * rows + off, CHUNK)
            here = pl.ds(off, CHUNK)
            inside = 1.0 - 0.25 * dist[at, :]
            unit = pair[at, :] * recip
            moved = unit * (dpair[at, :] - delta)
            dscore = inside * moved
            pull[at, :] += head_gamma * dscore + 0.5 * moved
            dscore_b = dscore.astype(jnp.bfloat16)
            attend_b = (inside * unit).astype(jnp.bfloat16)
            term = dot_nn(dscore_b, q) + dot_nn(attend_b, cot)
            kv = kv_refs[v][here, :]
            dq = dq + dot_tn(kv[:, : 2 * HEAD_DIM], dscore_b)
            gsum = gsum + dot_tn(kv[:, 2 * HEAD_DIM :], attend_b)
            high = term[:, 2 * HEAD_DIM :]
            vpos[at, :] += gates[at, :] * high
            extra = spread_groups(frames[at, :] * high)
            high = high + jnp.where(last_group, extra, 0.0)
            t_refs[v][here, : 2 * HEAD_DIM] = term[:, : 2 * HEAD_DIM].astype(t_refs[v].dtype)
            t_refs[v][here, 2 * HEAD_DIM :] = high.astype(t_refs[v].dtype)
            return dq, gsum

        dq, gsum = lax.fori_loop(0, chunks, graded, (dq, gsum), unroll=True)
    dq_ref[...] = (dq[:HEAD_DIM, :] * 0.125).astype(dq_ref.dtype)
    gsum = gsum[3 * VEC :, :]
    for c in range(3):
        part = ct_ref[0, c * VEC : (c + 1) * VEC, :].astype(jnp.float32) * gsum
        qpos[c : c + 1, :] -= jnp.sum(part, axis=0, keepdims=True)

    @pl.when(step == pl.num_programs(0) - 1)
    def _():
        def placed(k, sums):
            at = pl.ds(pl.multiple_of(k * CHUNK, CHUNK), CHUNK)
            kc = kc_ref[at, :]
            force = -2.0 * pull[at, :]
            vp = vpos[at, :]
            out = []
            cols = []
            for c in range(3):
                moment = force * (kc[:, c : c + 1] - qc_ref[c : c + 1, :])
                out.append(sums[c] - folded(moment))
                mine = (lane >= c * VEC) & (lane < (c + 1) * VEC)
                col = jnp.sum(moment, axis=1, keepdims=True)
                cols.append(col + jnp.sum(jnp.where(mine, vp, 0.0), axis=1, keepdims=True))
            kp_ref[at, :] = jnp.concatenate(cols + [jnp.zeros_like(cols[0])], axis=1)
            return tuple(out)

        zero = jnp.zeros((8, rows), jnp.float32)
        sums = lax.fori_loop(0, views * chunks, placed, (zero, zero, zero))
        qp_ref[...] = qpos[...]
        for c in range(3):
            qp_ref[c : c + 1, :] += jnp.sum(sums[c], axis=0, keepdims=True)


def head_group(gamma, q, cot, cot_t, query_coords, key_coords, blocks):
    heads, rows, _ = q.shape
    views = VIEWS
    keys = views * rows
    f32 = jnp.float32
    per_head = lambda h: (h, 0, 0)
    whole = lambda h: (0, 0)
    column = lambda h: (0, h)
    return pl.pallas_call(
        kernel,
        grid=(heads,),
        in_specs=[
            pl.BlockSpec(memory_space=pltpu.SMEM),
            pl.BlockSpec((1, rows, WIDTH), per_head),
            pl.BlockSpec((1, rows, WIDTH), per_head),
            pl.BlockSpec((1, 3 * VEC, rows), per_head),
            pl.BlockSpec(query_coords.shape, whole),
            pl.BlockSpec(key_coords.shape, whole),
        ]
        + [pl.BlockSpec((rows, WIDTH), column)] * views,
        out_specs=[pl.BlockSpec((rows, WIDTH), column)] * views
        + [
            pl.BlockSpec((HEAD_DIM, rows), lambda h: (h, 0)),
            pl.BlockSpec((keys, 4), whole),
            pl.BlockSpec((8, rows), whole),
        ],
        out_shape=[jax.ShapeDtypeStruct((rows, heads * WIDTH), jnp.bfloat16)] * views
        + [
            jax.ShapeDtypeStruct((heads * HEAD_DIM, rows), jnp.bfloat16),
            jax.ShapeDtypeStruct((keys, 4), f32),
            jax.ShapeDtypeStruct((8, rows), f32),
        ],
        scratch_shapes=[
            pltpu.VMEM((keys, rows), f32),
            pltpu.VMEM((keys, rows), f32),
            pltpu.VMEM((keys, rows), f32),
            pltpu.VMEM((keys, rows), f32),
            pltpu.VMEM((keys, 4 * VEC), f32),
            pltpu.VMEM((keys, 4 * VEC), f32),
            pltpu.VMEM((keys, 4 * VEC), f32),
            pltpu.VMEM((8, rows), f32),
        ],
        compiler_params=pltpu.CompilerParams(
            dimension_semantics=("arbitrary",), vmem_limit_bytes=60 * 2**20
        ),
        cost_estimate=pl.CostEstimate(
            flops=heads * rows * keys * 1500,
            bytes_accessed=heads * keys * WIDTH * 4,
            transcendentals=heads * rows * keys,
        ),
        name="pairs",
    )(gamma, q, cot, cot_t, query_coords, key_coords, *blocks)


def per_device(queries, key_values, out_grads, positions, counts, gamma):
    rows = queries.shape[0]
    heads = gamma.shape[0]
    groups = GROUPS if heads % GROUPS == 0 else 1
    size = heads // groups
    f32 = jnp.float32
    bf16 = jnp.bfloat16
    validity = (jnp.arange(rows, dtype=jnp.int32) < counts[0]).astype(f32)
    coords = jnp.concatenate([positions, validity[None, :]], axis=0)
    place = lax.axis_index("slab")
    core, side = place % 2, place // 2 % 2
    near = core == side
    far_step = jnp.where(side == 0, 2.0, -2.0).astype(f32)
    near_step = jnp.where(core == 0, 1.0, -1.0).astype(f32)
    shifts = [jnp.zeros((), f32), far_step, -far_step, near_step, -near_step]
    coord_views = fetched_views(coords, near)
    fetched = [
        fetched_views(key_values[:, g * size * WIDTH : (g + 1) * size * WIDTH], near)
        for g in range(groups)
    ]

    q = queries.reshape(rows, heads, HEAD_DIM).transpose(1, 0, 2) * bf16(0.125)
    q = jnp.pad(q, ((0, 0), (0, 0), (0, WIDTH - HEAD_DIM)))
    do = out_grads.reshape(rows, heads, COT).transpose(1, 0, 2).astype(f32)
    tail = jnp.zeros((heads, rows, VEC), f32)
    for c in range(3):
        at = HEAD_DIM + c * VEC
        tail = tail - coords[c][None, :, None] * do[:, :, at : at + VEC]
    cot = jnp.concatenate([do, tail], axis=2) * validity[None, :, None]
    cot = jnp.pad(cot, ((0, 0), (0, 0), (HEAD_DIM, 0))).astype(bf16)
    cot_t = cot[:, :, 2 * HEAD_DIM : 2 * HEAD_DIM + 3 * VEC].transpose(0, 2, 1)

    query_coords = jnp.pad(coords, ((0, 4), (0, 0)))
    first_row = jnp.array([1, 0, 0, 0], f32)[:, None]
    key_coords = jnp.concatenate(
        [view + shift * first_row for view, shift in zip(coord_views, shifts)], axis=1
    ).T

    dq_parts = []
    kv_parts = []
    key_pos = 0.0
    query_pos = 0.0
    for g in range(groups):
        part = slice(g * size, (g + 1) * size)
        out = head_group(
            gamma[part], q[part], cot[part], cot_t[part], query_coords, key_coords, fetched[g]
        )
        dq_parts.append(out[-3])
        key_pos = key_pos + out[-2]
        query_pos = query_pos + out[-1][:3]
        kv_parts.append(returned_terms(out[:VIEWS], near, bf16).astype(bf16))

    key_pos = key_pos.T[:3].reshape(3, VIEWS, rows)
    total = query_pos + returned_terms([key_pos[:, n] for n in range(VIEWS)], near, f32)
    position_grads = lax.psum(total, "head")
    query_grads = jnp.concatenate(dq_parts, axis=0).T
    return (query_grads, jnp.concatenate(kv_parts, axis=1), position_grads)


def solution(mesh):
    in_specs = (
        P("slab", "head"),
        P("slab", "head"),
        P("slab", "head"),
        P(None, "slab"),
        P("slab"),
        P("head"),
    )
    out_specs = (P("slab", "head"), P("slab", "head"), P(None, "slab"))
    return jax.shard_map(
        per_device, mesh=mesh, in_specs=in_specs, out_specs=out_specs, check_vma=False
    )
```

```python
import functools

import jax
import jax.numpy as jnp
from jax import lax
from jax.experimental import pallas as pl
from jax.experimental.pallas import tpu as pltpu
from jax.sharding import PartitionSpec as P

HEAD_DIM = 64
VEC = 32
WIDTH = 2 * HEAD_DIM + 4 * VEC
COT = HEAD_DIM + 3 * VEC
VIEWS = 5
FAR = 1e6
FLOOR = -1e4
CHUNK = 256
GROUPS = 2


def routed(block, axis, target):
    route = [(i, target(i) % lax.axis_size(axis)) for i in range(lax.axis_size(axis))]
    return lax.ppermute(block, axis, route)


def across_pairs(block):
    return routed(block, "slab", lambda i: i ^ 2)


def along_line(block, sign):
    return routed(block, "slab", lambda i: i + (sign if i & 2 == 0 else -sign) * 4)


def across_cores(block):
    return routed(block, "slab", lambda i: i ^ 1)


def fetched_views(block, near):
    far_one = across_pairs(block)
    far_two = along_line(far_one, 1)
    next_one = across_cores(block)
    next_two = across_cores(jnp.where(near, far_one, far_two))
    return [block, far_one, far_two, next_one, next_two]


def returned_terms(terms, near, dtype):
    f32 = jnp.float32
    own, far_one, far_two, next_one, next_two = terms
    swapped = across_cores(next_two).astype(f32)
    far_two = far_two.astype(f32) + jnp.where(near, 0.0, swapped)
    far_one = far_one.astype(f32) + jnp.where(near, swapped, 0.0)
    far_one = far_one + along_line(far_two.astype(dtype), -1).astype(f32)
    own = own.astype(f32) + across_cores(next_one).astype(f32)
    return own + across_pairs(far_one.astype(dtype)).astype(f32)


def dot_nt(a, b):
    return lax.dot_general(a, b, (((1,), (1,)), ((), ())), preferred_element_type=jnp.float32)


def dot_tn(a, b):
    return lax.dot_general(a, b, (((0,), (0,)), ((), ())), preferred_element_type=jnp.float32)


def dot_nn(a, b):
    return jnp.dot(a, b, preferred_element_type=jnp.float32)


def spread_groups(x):
    x = x + pltpu.roll(x, 2 * VEC, 1)
    return x + pltpu.roll(x, VEC, 1)


def folded(x):
    return jnp.sum(x.reshape(x.shape[0] // 8, 8, x.shape[1]), axis=0)


def kernel(gamma_ref, q_ref, c_ref, ct_ref, qc_ref, kc_ref, *rest):
    views = VIEWS
    kv_refs = rest[:views]
    t_refs = rest[views : 2 * views]
    dq_ref, kp_ref, qp_ref = rest[2 * views : 2 * views + 3]
    dist, pair, dpair, pull, gates, frames, vpos, qpos = rest[2 * views + 3 :]
    rows = q_ref.shape[1]
    chunks = rows // CHUNK
    step = pl.program_id(0)
    head_gamma = gamma_ref[step]
    lane = lax.broadcasted_iota(jnp.int32, (CHUNK, 4 * VEC), 1)
    last_group = lane >= 3 * VEC

    @pl.when(step == 0)
    def _():
        vpos[...] = jnp.zeros_like(vpos)
        qpos[...] = jnp.zeros_like(qpos)

        @pl.loop(0, views * chunks)
        def _(k):
            at = pl.ds(pl.multiple_of(k * CHUNK, CHUNK), CHUNK)
            kc = kc_ref[at, :]
            total = None
            for c in range(3):
                shift = kc[:, c : c + 1] - qc_ref[c : c + 1, :]
                total = shift * shift if total is None else total + shift * shift
            counted = (1.0 - total * 0.25 > 0.0) & (kc[:, 3:4] > 0.5)
            dist[at, :] = jnp.where(counted, total, FAR)
            pull[at, :] = jnp.zeros((CHUNK, rows), jnp.float32)
            frames[at, :] = jnp.where(
                lane < VEC,
                kc[:, 0:1],
                jnp.where(lane < 2 * VEC, kc[:, 1:2], jnp.where(last_group, 0.0, kc[:, 2:3])),
            )

    q = q_ref[0]
    cot = c_ref[0]
    peak = jnp.full((8, rows), FLOOR, jnp.float32)
    for v in range(views):

        def scored(k, peak, v=v):
            off = pl.multiple_of(k * CHUNK, CHUNK)
            at = pl.ds(v * rows + off, CHUNK)
            s = dot_nt(kv_refs[v][pl.ds(off, CHUNK), : 2 * HEAD_DIM], q[:, : 2 * HEAD_DIM])
            s = s - head_gamma * dist[at, :]
            pair[at, :] = s
            return jnp.maximum(peak, jnp.max(s.reshape(CHUNK // 8, 8, rows), axis=0))

        peak = lax.fori_loop(0, chunks, scored, peak, unroll=True)
    peak = jnp.max(peak, axis=0, keepdims=True)

    totals = jnp.zeros((8, rows), jnp.float32)
    weighted = jnp.zeros((8, rows), jnp.float32)
    for v in range(views):

        def summed(k, carry, v=v):
            totals, weighted = carry
            off = pl.multiple_of(k * CHUNK, CHUNK)
            at = pl.ds(v * rows + off, CHUNK)
            kv = kv_refs[v][pl.ds(off, CHUNK), :]
            high = kv[:, 2 * HEAD_DIM :].astype(jnp.float32)
            gate = spread_groups(jnp.where(last_group, high, 0.0))
            gates[at, :] = gate
            primed = (high + frames[at, :] * gate).astype(jnp.bfloat16)
            dp = dot_nt(kv[:, : 2 * HEAD_DIM], cot[:, : 2 * HEAD_DIM]) + dot_nt(
                primed, cot[:, 2 * HEAD_DIM :]
            )
            inside = 1.0 - 0.25 * dist[at, :]
            part = inside * jnp.exp(pair[at, :] - peak)
            pair[at, :] = part
            dpair[at, :] = dp
            weight = inside * part
            return totals + folded(weight), weighted + folded(weight * dp)

        totals, weighted = lax.fori_loop(0, chunks, summed, (totals, weighted), unroll=True)
    total = jnp.sum(totals, axis=0, keepdims=True) + (1.0 - qc_ref[3:4, :])
    recip = 1.0 / total
    delta = jnp.sum(weighted, axis=0, keepdims=True) / total

    dq = jnp.zeros((2 * HEAD_DIM, rows), jnp.float32)
    gsum = jnp.zeros((4 * VEC, rows), jnp.float32)
    for v in range(views):

        def graded(k, carry, v=v):
            dq, gsum = carry
            off = pl.multiple_of(k * CHUNK, CHUNK)
            at = pl.ds(v * rows + off, CHUNK)
            here = pl.ds(off, CHUNK)
            inside = 1.0 - 0.25 * dist[at, :]
            unit = pair[at, :] * recip
            moved = unit * (dpair[at, :] - delta)
            dscore = inside * moved
            pull[at, :] += head_gamma * dscore + 0.5 * moved
            dscore_b = dscore.astype(jnp.bfloat16)
            attend_b = (inside * unit).astype(jnp.bfloat16)
            term = dot_nn(dscore_b, q) + dot_nn(attend_b, cot)
            kv = kv_refs[v][here, :]
            dq = dq + dot_tn(kv[:, : 2 * HEAD_DIM], dscore_b)
            gsum = gsum + dot_tn(kv[:, 2 * HEAD_DIM :], attend_b)
            high = term[:, 2 * HEAD_DIM :]
            vpos[at, :] += gates[at, :] * high
            extra = spread_groups(frames[at, :] * high)
            high = high + jnp.where(last_group, extra, 0.0)
            t_refs[v][here, : 2 * HEAD_DIM] = term[:, : 2 * HEAD_DIM].astype(t_refs[v].dtype)
            t_refs[v][here, 2 * HEAD_DIM :] = high.astype(t_refs[v].dtype)
            return dq, gsum

        dq, gsum = lax.fori_loop(0, chunks, graded, (dq, gsum), unroll=True)
    dq_ref[...] = (dq[:HEAD_DIM, :] * 0.125).astype(dq_ref.dtype)
    gsum = gsum[3 * VEC :, :]
    for c in range(3):
        part = ct_ref[0, c * VEC : (c + 1) * VEC, :].astype(jnp.float32) * gsum
        qpos[c : c + 1, :] -= jnp.sum(part, axis=0, keepdims=True)

    @pl.when(step == pl.num_programs(0) - 1)
    def _():
        def placed(k, sums):
            at = pl.ds(pl.multiple_of(k * CHUNK, CHUNK), CHUNK)
            kc = kc_ref[at, :]
            force = -2.0 * pull[at, :]
            vp = vpos[at, :]
            out = []
            cols = []
            for c in range(3):
                moment = force * (kc[:, c : c + 1] - qc_ref[c : c + 1, :])
                out.append(sums[c] - folded(moment))
                mine = (lane >= c * VEC) & (lane < (c + 1) * VEC)
                col = jnp.sum(moment, axis=1, keepdims=True)
                cols.append(col + jnp.sum(jnp.where(mine, vp, 0.0), axis=1, keepdims=True))
            kp_ref[at, :] = jnp.concatenate(cols + [jnp.zeros_like(cols[0])], axis=1)
            return tuple(out)

        zero = jnp.zeros((8, rows), jnp.float32)
        sums = lax.fori_loop(0, views * chunks, placed, (zero, zero, zero))
        qp_ref[...] = qpos[...]
        for c in range(3):
            qp_ref[c : c + 1, :] += jnp.sum(sums[c], axis=0, keepdims=True)


def head_group(gamma, q, cot, cot_t, query_coords, key_coords, blocks):
    heads, rows, _ = q.shape
    views = VIEWS
    keys = views * rows
    f32 = jnp.float32
    per_head = lambda h: (h, 0, 0)
    whole = lambda h: (0, 0)
    column = lambda h: (0, h)
    return pl.pallas_call(
        kernel,
        grid=(heads,),
        in_specs=[
            pl.BlockSpec(memory_space=pltpu.SMEM),
            pl.BlockSpec((1, rows, WIDTH), per_head),
            pl.BlockSpec((1, rows, WIDTH), per_head),
            pl.BlockSpec((1, 3 * VEC, rows), per_head),
            pl.BlockSpec(query_coords.shape, whole),
            pl.BlockSpec(key_coords.shape, whole),
        ]
        + [pl.BlockSpec((rows, WIDTH), column)] * views,
        out_specs=[pl.BlockSpec((rows, WIDTH), column)] * views
        + [
            pl.BlockSpec((HEAD_DIM, rows), lambda h: (h, 0)),
            pl.BlockSpec((keys, 4), whole),
            pl.BlockSpec((8, rows), whole),
        ],
        out_shape=[jax.ShapeDtypeStruct((rows, heads * WIDTH), jnp.bfloat16)] * views
        + [
            jax.ShapeDtypeStruct((heads * HEAD_DIM, rows), jnp.bfloat16),
            jax.ShapeDtypeStruct((keys, 4), f32),
            jax.ShapeDtypeStruct((8, rows), f32),
        ],
        scratch_shapes=[
            pltpu.VMEM((keys, rows), f32),
            pltpu.VMEM((keys, rows), f32),
            pltpu.VMEM((keys, rows), f32),
            pltpu.VMEM((keys, rows), f32),
            pltpu.VMEM((keys, 4 * VEC), f32),
            pltpu.VMEM((keys, 4 * VEC), f32),
            pltpu.VMEM((keys, 4 * VEC), f32),
            pltpu.VMEM((8, rows), f32),
        ],
        compiler_params=pltpu.CompilerParams(
            dimension_semantics=("arbitrary",), vmem_limit_bytes=60 * 2**20
        ),
        cost_estimate=pl.CostEstimate(
            flops=heads * rows * keys * 10000,
            bytes_accessed=heads * keys * WIDTH * 4,
            transcendentals=heads * rows * keys,
        ),
        name="pairs",
    )(gamma, q, cot, cot_t, query_coords, key_coords, *blocks)


def per_device(queries, key_values, out_grads, positions, counts, gamma):
    rows = queries.shape[0]
    heads = gamma.shape[0]
    groups = GROUPS if heads % GROUPS == 0 else 1
    size = heads // groups
    f32 = jnp.float32
    bf16 = jnp.bfloat16
    validity = (jnp.arange(rows, dtype=jnp.int32) < counts[0]).astype(f32)
    coords = jnp.concatenate([positions, validity[None, :]], axis=0)
    place = lax.axis_index("slab")
    core, side = place % 2, place // 2 % 2
    near = core == side
    far_step = jnp.where(side == 0, 2.0, -2.0).astype(f32)
    near_step = jnp.where(core == 0, 1.0, -1.0).astype(f32)
    shifts = [jnp.zeros((), f32), far_step, -far_step, near_step, -near_step]
    coord_views = fetched_views(coords, near)
    fetched = [
        fetched_views(key_values[:, g * size * WIDTH : (g + 1) * size * WIDTH], near)
        for g in range(groups)
    ]

    q = queries.reshape(rows, heads, HEAD_DIM).transpose(1, 0, 2) * bf16(0.125)
    q = jnp.pad(q, ((0, 0), (0, 0), (0, WIDTH - HEAD_DIM)))
    do = out_grads.reshape(rows, heads, COT).transpose(1, 0, 2).astype(f32)
    tail = jnp.zeros((heads, rows, VEC), f32)
    for c in range(3):
        at = HEAD_DIM + c * VEC
        tail = tail - coords[c][None, :, None] * do[:, :, at : at + VEC]
    cot = jnp.concatenate([do, tail], axis=2) * validity[None, :, None]
    cot = jnp.pad(cot, ((0, 0), (0, 0), (HEAD_DIM, 0))).astype(bf16)
    cot_t = cot[:, :, 2 * HEAD_DIM : 2 * HEAD_DIM + 3 * VEC].transpose(0, 2, 1)

    query_coords = jnp.pad(coords, ((0, 4), (0, 0)))
    first_row = jnp.array([1, 0, 0, 0], f32)[:, None]
    key_coords = jnp.concatenate(
        [view + shift * first_row for view, shift in zip(coord_views, shifts)], axis=1
    ).T

    dq_parts = []
    kv_parts = []
    key_pos = 0.0
    query_pos = 0.0
    for g in range(groups):
        part = slice(g * size, (g + 1) * size)
        out = head_group(
            gamma[part], q[part], cot[part], cot_t[part], query_coords, key_coords, fetched[g]
        )
        dq_parts.append(out[-3])
        key_pos = key_pos + out[-2]
        query_pos = query_pos + out[-1][:3]
        kv_parts.append(returned_terms(out[:VIEWS], near, bf16).astype(bf16))

    key_pos = key_pos.T[:3].reshape(3, VIEWS, rows)
    total = query_pos + returned_terms([key_pos[:, n] for n in range(VIEWS)], near, f32)
    position_grads = lax.psum(total, "head")
    query_grads = jnp.concatenate(dq_parts, axis=0).T
    return (query_grads, jnp.concatenate(kv_parts, axis=1), position_grads)


def solution(mesh):
    in_specs = (
        P("slab", "head"),
        P("slab", "head"),
        P("slab", "head"),
        P(None, "slab"),
        P("slab"),
        P("head"),
    )
    out_specs = (P("slab", "head"), P("slab", "head"), P(None, "slab"))
    return jax.shard_map(
        per_device, mesh=mesh, in_specs=in_specs, out_specs=out_specs, check_vma=False
    )
```
